128 devices in a mesh: fsdp: 8 (over x_lo, y), tp: 16 (over z, x_hi, core).
Axes of the slice: x: 4 (x_hi: 2, x_lo: 2; x = x_hi * 2 + x_lo), y: 4, z: 4, core: 2. Of those that a mesh axis runs over, the one named last changes fastest.
Arguments:
- prefix_states: bfloat16 [32768, 8192], P('fsdp', 'tp'), may hold values from -40 to 40
- new_states: bfloat16 [128, 8192], P('fsdp', 'tp'), may hold values from -40 to 40
- w_query: bfloat16 [8192, 8192], P('tp', 'fsdp'), may hold values from -0.09375 to 0.09375
- w_keyvalue: bfloat16 [8192, 2048], P('tp', 'fsdp'), may hold values from -0.03125 to 0.03125
- w_output: bfloat16 [8192, 8192], P('tp', 'fsdp'), may hold values from -0.25 to 0.25
- lengths: int32 [8, 4], P('fsdp'), may hold values from 1 to 1024, 3072 in all within a row
Outputs:
- kv_cache: bfloat16 [32768, 2048], P('fsdp', 'tp')
- mixed: bfloat16 [128, 8192], P('fsdp', 'tp')
The draws below stay inside these ranges and needn't reach their ends.
Inputs may be any that keep to these rules, and one draw needn't show every extreme that they name: `lengths`: in every group some sequence has length 1024.
All inputs are finite; a program needn't handle non-finite values.
Results may differ from the reference program's by a relative error of at most 0.02.
Values may be sent and summed in bfloat16 or wider, within the bound.
No kernel may reach another device: no remote copies, remote signals or barrier semaphores. Data moves between devices by JAX's collectives and lax.ppermute only.
A program may use at most 128 MiB of HBM per device.

```python
import math
import jax
import jax.numpy as jnp
import numpy as np
from jax import lax

D = 8192
HQ = 64
KVH = 8
HD = 128
NSEQ = 4
L = 1024
STEPS = 4
GROUPS = 8
PREFIX_ROWS = 32768
FRESH_ROWS = 128
N_FSDP = 8
N_TP = 16


def draw_states(key, row_count, salt_value):
    noise_key = jax.random.fold_in(key, salt_value)
    values = jax.random.normal(jax.random.fold_in(noise_key, 4), (row_count, D), jnp.float32)
    return jnp.clip(values, -40.0, 40.0).astype(jnp.bfloat16)


def draw_prefix_states(key, part):
    return draw_states(key, PREFIX_ROWS, 101)


def draw_new_states(key, part):
    return draw_states(key, FRESH_ROWS, 202)


def with_spikes(drawn, own_key, source, target, blocks, factor):
    def block_of(dim):
        return (jnp.arange(drawn.shape[dim]) // (drawn.shape[dim] // blocks)).reshape((-1,) + (1,) * (drawn.ndim - 1 - dim))

    near = jax.random.permutation(own_key, blocks)[block_of(target)]
    far = (block_of(target) + blocks // 2) % blocks
    return jnp.where((block_of(source) == near) | (block_of(source) == far), factor * drawn, drawn)


def level_of(own_key, extent, cuts, low, high):
    gain = 1.0
    for position, parts in cuts:
        draws = jax.random.uniform(jax.random.fold_in(jax.random.fold_in(own_key, 6), position), (parts,), jnp.float32, low / len(cuts), high / len(cuts))
        gain = gain * jnp.repeat(jnp.exp(draws), extent[position] // parts).reshape((-1,) + (1,) * (len(extent) - 1 - position))
    return gain


def length_profile(number_of, total, bound, slope):
    weights = [(1 << 20) // math.isqrt(grade ** slope) + 1 for grade in range(2, number_of + 1)]
    spare, given = total - bound - (number_of - 1), [1] * (number_of - 1)
    while spare > 0:
        movable = [i for i in range(number_of - 1) if given[i] < bound]
        mass, remaining = sum([weights[i] for i in movable]), spare
        for i in movable:
            addition = min(bound - given[i], max(1, remaining * weights[i] // mass), spare)
            given[i] = given[i] + addition
            spare = spare - addition
    return np.array([bound] + given)


def ragged(key, number_of, total, most, lean):
    if number_of == 2:
        one = jax.random.randint(key, (), max(1, total - most), min(most, total - 1) + 1)
        return jnp.stack([one, total - one])
    sizes = jnp.asarray(length_profile(number_of, total, most, lean), jnp.int32)
    pairs = (number_of - 1) // 2
    donor, taker = sizes[1:1 + 2 * pairs:2], sizes[2:2 + 2 * pairs:2]
    margin = jnp.minimum(donor - 1, most - taker)
    passed = jax.random.randint(jax.random.fold_in(key, 1), (pairs,), 0, 1 << 20) % (margin + 1)
    sizes = sizes.at[1:1 + 2 * pairs:2].set(donor - passed).at[2:2 + 2 * pairs:2].set(taker + passed)
    return sizes[jax.random.permutation(jax.random.fold_in(key, 2), number_of)]


def bell_draw_with(stream_key, extent, spread, reach, pieces, heavy, kind=jnp.bfloat16):
    values = spread * jax.random.normal(stream_key, extent, jnp.float32)
    if pieces:
        values = values * level_of(stream_key, extent, pieces, -0.22, 0.18)
    return jnp.clip(with_spikes(values, jax.random.fold_in(stream_key, 3), *heavy), -reach, reach).astype(kind)


def setup_inputs(seed: int = 0) -> dict:
    seeds = jax.random.split(jax.random.key(seed), 7)
    prefix_states = draw_prefix_states(jax.random.fold_in(seeds[6], 71), 0)
    new_states = draw_new_states(jax.random.fold_in(seeds[6], 71), 0)
    w_query = bell_draw_with(seeds[2], (D, HQ * HD), D ** -0.5, 0.09375, ((0, 16), (1, 8)), (0, 1, 16, 2.0))
    w_keyvalue = bell_draw_with(seeds[3], (D, 2 * KVH * HD), (8 * D) ** -0.5, 0.03125, ((0, 16), (1, 8)), (0, 1, 16, 2.0))
    w_output = bell_draw_with(seeds[4], (HQ * HD, D), (HQ * HD // 8) ** -0.5, 0.25, ((0, 16), (1, 8)), (0, 1, 16, 2.0))
    lengths = jax.vmap(lambda own: ragged(own, NSEQ, 3 * NSEQ * L // 4, L, 1))(jax.random.split(seeds[5], GROUPS)).reshape((GROUPS, NSEQ)).astype(jnp.int32)
    return dict(prefix_states=prefix_states, new_states=new_states, w_query=w_query, w_keyvalue=w_keyvalue, w_output=w_output, lengths=lengths)


theta_base = 500000.0


def rotate(values, positions):
    half_dim = values.shape[-1] // 2
    frequency = theta_base ** (-2.0 * jnp.arange(half_dim, dtype=jnp.float32) / values.shape[-1])
    angles = positions[:, None, None] * frequency[None, None, :]
    cosine = jnp.cos(angles)
    sine_part = jnp.sin(angles)
    lower_half = values[..., :half_dim]
    upper_half = values[..., half_dim:]
    return jnp.concatenate([lower_half * cosine - upper_half * sine_part, upper_half * cosine + lower_half * sine_part], axis=-1)


def one_group(prefix_rows, fresh_rows, seq_lengths, w_query, w_keyvalue, w_output):
    token_count = prefix_rows.shape[0]
    fresh_count = fresh_rows.shape[0]
    block_width = D // N_TP
    kv_total = jnp.zeros((token_count, 2 * KVH * HD), jnp.float32)
    for block_index in range(N_TP):
        low_edge = block_index * block_width
        partial_kv = jnp.dot(prefix_rows[:, low_edge:low_edge + block_width], w_keyvalue[low_edge:low_edge + block_width], preferred_element_type=jnp.float32)
        kv_total = kv_total + lax.optimization_barrier(partial_kv.astype(jnp.bfloat16)).astype(jnp.float32)
    kv_heads = kv_total.reshape(token_count, KVH, 2, HD)
    slot_positions = (jnp.arange(token_count, dtype=jnp.int32) % L).astype(jnp.float32)
    rotated_keys = rotate(kv_heads[:, :, 0, :], slot_positions)
    cache = jnp.stack([rotated_keys, kv_heads[:, :, 1, :]], axis=2).reshape(token_count, 2 * KVH * HD).astype(jnp.bfloat16)
    query_sum = jnp.dot(fresh_rows, w_query, preferred_element_type=jnp.float32)
    new_kv = jnp.dot(fresh_rows, w_keyvalue, preferred_element_type=jnp.float32).reshape(fresh_count, KVH, 2, HD)
    fresh_positions = (jnp.repeat(seq_lengths, STEPS) + jnp.tile(jnp.arange(STEPS, dtype=jnp.int32), NSEQ)).astype(jnp.float32)
    query = rotate(query_sum.reshape(fresh_count, HQ, HD), fresh_positions).astype(jnp.bfloat16)
    new_keys = rotate(new_kv[:, :, 0, :], fresh_positions).astype(jnp.bfloat16)
    new_values = new_kv[:, :, 1, :].astype(jnp.bfloat16)
    cache_heads = cache.reshape(NSEQ, L, KVH, 2, HD).astype(jnp.float32)
    prefix_keys = cache_heads[:, :, :, 0, :]
    prefix_values = cache_heads[:, :, :, 1, :]
    query_five = query.astype(jnp.float32).reshape(NSEQ, STEPS, KVH, HQ // KVH, HD)
    score_scale = HD ** -0.5
    prefix_scores = jnp.einsum('sjkgd,slkd->sjkgl', query_five, prefix_keys, precision=lax.Precision.HIGHEST) * score_scale
    live_keys = jnp.arange(L, dtype=jnp.int32)[None, :] < seq_lengths[:, None]
    prefix_scores = jnp.where(live_keys[:, None, None, None, :], prefix_scores, -jnp.inf)
    fresh_keys = new_keys.astype(jnp.float32).reshape(NSEQ, STEPS, KVH, HD)
    fresh_values = new_values.astype(jnp.float32).reshape(NSEQ, STEPS, KVH, HD)
    fresh_scores = jnp.einsum('sjkgd,sikd->sjkgi', query_five, fresh_keys, precision=lax.Precision.HIGHEST) * score_scale
    causal = jnp.arange(STEPS)[None, :] <= jnp.arange(STEPS)[:, None]
    fresh_scores = jnp.where(causal[None, :, None, None, :], fresh_scores, -jnp.inf)
    row_max = jnp.maximum(jnp.max(prefix_scores, axis=-1), jnp.max(fresh_scores, axis=-1))
    prefix_weight = jnp.exp(prefix_scores - row_max[..., None])
    fresh_weight = jnp.exp(fresh_scores - row_max[..., None])
    denominator = jnp.sum(prefix_weight, axis=-1) + jnp.sum(fresh_weight, axis=-1)
    prefix_rounded = lax.optimization_barrier(prefix_weight.astype(jnp.bfloat16)).astype(jnp.float32)
    fresh_rounded = lax.optimization_barrier(fresh_weight.astype(jnp.bfloat16)).astype(jnp.float32)
    numerator = jnp.einsum('sjkgl,slkd->sjkgd', prefix_rounded, prefix_values, precision=lax.Precision.HIGHEST)
    numerator = numerator + jnp.einsum('sjkgi,sikd->sjkgd', fresh_rounded, fresh_values, precision=lax.Precision.HIGHEST)
    attended = (numerator / denominator[..., None]).reshape(fresh_count, HQ * HD).astype(jnp.bfloat16)
    mixed = jnp.dot(attended, w_output, preferred_element_type=jnp.float32).astype(jnp.bfloat16)
    return cache, mixed


def reference(prefix_states, new_states, w_query, w_keyvalue, w_output, lengths):
    prefix_groups = prefix_states.reshape(N_FSDP, NSEQ * L, D)
    fresh_groups = new_states.reshape(N_FSDP, NSEQ * STEPS, D)

    def run_group(packed):
        return one_group(packed[0], packed[1], packed[2], w_query, w_keyvalue, w_output)

    caches, outputs = lax.map(run_group, (prefix_groups, fresh_groups, lengths))
    return caches.reshape(N_FSDP * NSEQ * L, 2 * KVH * HD), outputs.reshape(N_FSDP * NSEQ * STEPS, D)
```

```python
import functools

import jax
import jax.numpy as jnp
from jax import lax
from jax.experimental import pallas as pl
from jax.experimental.pallas import tpu as pltpu
from jax.sharding import PartitionSpec as P

HD = 128
NSEQ = 4
L = 1024
STEPS = 4
N_FSDP = 8
N_TP = 16
ROWS = NSEQ * STEPS


theta_base = 500000.0
masked_score = -1e30
both = ("fsdp", "tp")
f32 = jnp.float32
bf16 = jnp.bfloat16

Z_FIRST = 2560
Z_TILE = 640
X_TILE = 512


def route(move):
    pairs = []
    for f in range(N_FSDP):
        for t in range(N_TP):
            a, b = move(f, t)
            pairs.append((f * N_TP + t, a * N_TP + b))
    return pairs


def to_core(block):
    return lax.ppermute(block, both, route(lambda f, t: (f, t ^ 1)))


def to_x(block):
    return lax.ppermute(block, both, route(lambda f, t: (f, t ^ 2)))


def to_z(block, step):
    return lax.ppermute(
        block, both, route(lambda f, t: (f, (((t >> 2) + step) % 4) << 2 | (t & 3)))
    )


def to_group(block, flip):
    return lax.ppermute(block, both, route(lambda f, t: (f ^ flip, t)))


def transpose_mesh(block):
    return lax.ppermute(block, both, route(lambda f, t: (t >> 1, 2 * f + (t & 1))))


def partial_kernel(heads, slots, x1, x2, *rest):
    weights, out, merged = rest[:heads], rest[heads], rest[heads + 1]

    @pl.when(pl.program_id(0) == 0)
    def _():
        for j in range(heads):
            merged[:, j * HD : (j + 1) * HD] = weights[j][0]

    depth = x1.shape[1]
    total = jnp.dot(x1[...], merged[:depth, :], preferred_element_type=f32)
    total = total + jnp.dot(x2[...], merged[depth:, :], preferred_element_type=f32)
    out[...] = total.astype(bf16)


def partial_heads(x1, x2, weights, slots, start, rows, tile):
    heads = slots.shape[0]
    depth = x1.shape[1]
    first = start // tile
    x_spec = pl.BlockSpec((tile, depth), lambda i, s: (first + i, 0))
    w_specs = [
        pl.BlockSpec((1, 2 * depth, HD), lambda i, s, j=j: (s[j], 0, 0)) for j in range(heads)
    ]
    width = heads * HD
    return pl.pallas_call(
        functools.partial(partial_kernel, heads),
        out_shape=jax.ShapeDtypeStruct((rows, width), bf16),
        grid_spec=pltpu.PrefetchScalarGridSpec(
            num_scalar_prefetch=1,
            grid=(rows // tile,),
            in_specs=[x_spec, x_spec] + w_specs,
            out_specs=pl.BlockSpec((tile, width), lambda i, s: (i, 0)),
            scratch_shapes=[pltpu.VMEM((2 * depth, width), bf16)],
        ),
        cost_estimate=pl.CostEstimate(
            flops=4 * rows * depth * width,
            bytes_accessed=2 * (2 * rows * depth + 2 * depth * width + rows * width),
            transcendentals=0,
        ),
        name="partial_heads",
    )(slots, x1, x2, *([weights] * heads))


def fresh_kernel(group, packed, w_query, w_keyvalue, out, rows_ref):
    for a in range(N_FSDP):
        slot = a ^ group[0]
        for j in range(4):
            rows_ref[a * ROWS : (a + 1) * ROWS, j * HD : (j + 1) * HD] = packed[
                slot, j * ROWS : (j + 1) * ROWS, :
            ]
    rows = rows_ref[...]
    query = jnp.dot(rows, w_query[...], preferred_element_type=f32)
    keyvalue = jnp.dot(rows, w_keyvalue[...], preferred_element_type=f32)
    for a in range(N_FSDP):
        for h in range(2):
            low = a * ROWS
            out[2 * a + h, :, :512] = query[low : low + ROWS, h * 512 : (h + 1) * 512]
            out[2 * a + h, :, 512:] = keyvalue[low : low + ROWS, h * HD : (h + 1) * HD]


def fresh_terms(group, packed, w_query, w_keyvalue):
    whole = lambda shape: pl.BlockSpec(shape, lambda i, s: (0,) * len(shape))
    return pl.pallas_call(
        fresh_kernel,
        out_shape=jax.ShapeDtypeStruct((N_TP, ROWS, 640), f32),
        grid_spec=pltpu.PrefetchScalarGridSpec(
            num_scalar_prefetch=1,
            grid=(1,),
            in_specs=[
                pl.BlockSpec((N_FSDP, 64, HD), lambda i, s: (0, 16, 0)),
                whole((512, 1024)),
                whole((512, 256)),
            ],
            out_specs=whole((N_TP, ROWS, 640)),
            scratch_shapes=[pltpu.VMEM((N_FSDP * ROWS, 512), bf16)],
        ),
        cost_estimate=pl.CostEstimate(
            flops=2 * 128 * 512 * 1280, bytes_accessed=2 << 20, transcendentals=0
        ),
        name="fresh_terms",
    )(group, packed, w_query, w_keyvalue)


def output_kernel(attended, w_output, out):
    rows = attended[...].reshape(N_FSDP * ROWS, 512)
    total = jnp.dot(rows, w_output[...], preferred_element_type=f32)
    for a in range(N_FSDP):
        for h in range(2):
            out[2 * a + h] = total[a * ROWS : (a + 1) * ROWS, h * 512 : (h + 1) * 512]


def output_terms(attended, w_output):
    return pl.pallas_call(
        output_kernel,
        out_shape=jax.ShapeDtypeStruct((N_TP, ROWS, 512), f32),
        in_specs=[pl.BlockSpec(memory_space=pltpu.VMEM)] * 2,
        out_specs=pl.BlockSpec(memory_space=pltpu.VMEM),
        name="output_terms",
    )(attended, w_output)


def finish_kernel(z_rows, z_own, z_in, xa, xb, cosine, sine, out):
    def rotated(total, low):
        table = pl.ds(low % L, total.shape[0])
        return (total * cosine[table, :] + pltpu.roll(total, HD // 2, 1) * sine[table, :]).astype(
            bf16
        )

    step = 256
    half = xa.shape[0]
    for low in range(0, z_rows, step):
        rows = slice(low, low + step)
        out[rows, :] = rotated(z_own[rows, :].astype(f32) + z_in[rows, :].astype(f32), low)
    for ref, base in ((xa, z_rows), (xb, z_rows + half)):
        for low in range(0, half, step):
            out[base + low : base + low + step, :] = rotated(
                ref[low : low + step, :].astype(f32), base + low
            )


def finish_cache(z_own, z_in, xa, xb, cosine, sine):
    z_rows = z_own.shape[0]
    return pl.pallas_call(
        functools.partial(finish_kernel, z_rows),
        out_shape=jax.ShapeDtypeStruct((NSEQ * L, HD), bf16),
        in_specs=[pl.BlockSpec(memory_space=pltpu.VMEM)] * 6,
        out_specs=pl.BlockSpec(memory_space=pltpu.VMEM),
        name="finish_cache",
    )(z_own, z_in, xa, xb, cosine, sine)


def attention_kernel(info, mine, other, fresh_mine, fresh_other, query, out):
    holds_keys = info[NSEQ] == 0
    scale = HD ** (-0.5)
    fresh_keys = jnp.where(holds_keys, fresh_mine[...], fresh_other[...])
    fresh_values = jnp.where(holds_keys, fresh_other[...], fresh_mine[...])
    for s in range(NSEQ):
        part = slice(s * L, (s + 1) * L)
        keys = jnp.where(holds_keys, mine[part, :], other[part, :])
        values = jnp.where(holds_keys, other[part, :], mine[part, :])
        rows = query[s * 16 : (s + 1) * 16, :]
        last = (((1,), (1,)), ((), ()))
        scores = lax.dot_general(rows, keys, last, preferred_element_type=f32) * scale
        slot = lax.broadcasted_iota(jnp.int32, scores.shape, 1)
        scores = jnp.where(slot < info[s], scores, masked_score)
        fresh = lax.dot_general(rows, fresh_keys, last, preferred_element_type=f32) * scale
        row = lax.broadcasted_iota(jnp.int32, fresh.shape, 0)
        column = lax.broadcasted_iota(jnp.int32, fresh.shape, 1)
        step = column - s * STEPS
        live = (step >= 0) & (step <= (row >> 2))
        fresh = jnp.where(live, fresh, masked_score)
        top = jnp.maximum(
            jnp.max(scores, axis=1, keepdims=True), jnp.max(fresh, axis=1, keepdims=True)
        )
        weight = jnp.exp(scores - top)
        fresh_weight = jnp.exp(fresh - top)
        denominator = jnp.sum(weight, axis=1, keepdims=True) + jnp.sum(
            fresh_weight, axis=1, keepdims=True
        )
        numerator = jnp.dot(weight.astype(bf16), values, preferred_element_type=f32)
        numerator = numerator + jnp.dot(
            fresh_weight.astype(bf16), fresh_values, preferred_element_type=f32
        )
        out[s * 16 : (s + 1) * 16, :] = (numerator / denominator).astype(bf16)


def attend(info, mine, other, fresh_mine, fresh_other, query):
    vmem = pl.BlockSpec(memory_space=pltpu.VMEM)
    return pl.pallas_call(
        attention_kernel,
        out_shape=jax.ShapeDtypeStruct((64, HD), bf16),
        in_specs=[pl.BlockSpec(memory_space=pltpu.SMEM)] + [vmem] * 5,
        out_specs=vmem,
        name="attend",
    )(info, mine, other, fresh_mine, fresh_other, query)


def rotate(values, cosine, sine):
    return values * cosine + jnp.roll(values, HD // 2, axis=-1) * sine


def tables(positions):
    half = HD // 2
    frequency = theta_base ** (-2.0 * jnp.arange(half, dtype=f32) / HD)
    angles = positions[:, None] * frequency[None, :]
    cosine, sine = jnp.cos(angles), jnp.sin(angles)
    return jnp.concatenate([cosine, cosine], 1), jnp.concatenate([-sine, sine], 1)


def add(*blocks):
    total = blocks[0].astype(f32)
    for block in blocks[1:]:
        total = total + block.astype(f32)
    return total.astype(bf16)


def reduce_over_z(far_a, far_b, up_a, up_b, down_a, down_b, own_a, own_b):
    in_far_a = to_z(far_a, 1)
    in_far_b = to_z(far_b, -1)
    in_up_b = to_z(up_b, 1)
    in_down_a = to_z(down_a, -1)
    in_up_a = to_z(add(up_a, in_far_a), 1)
    in_down_b = to_z(add(down_b, in_far_b), -1)
    return (own_a, in_down_a, in_up_a), (own_b, in_up_b, in_down_b)


def body(prefix_states, new_states, w_query, w_keyvalue, w_output, lengths):
    group = lax.axis_index("fsdp")
    me = lax.axis_index("tp")
    z, x, core = me >> 2, (me >> 1) & 1, me & 1
    slots = prefix_states.shape[0]
    holds_keys = core == 0

    lower, upper = w_keyvalue[:, :HD], w_keyvalue[:, HD:]
    kept = jnp.where(holds_keys, lower, upper)
    given = jnp.where(holds_keys, upper, lower)
    got = to_core(given)
    other_states = to_core(prefix_states)
    packed_rows = new_states.reshape(ROWS, 4, HD).transpose(1, 0, 2).reshape(4 * ROWS, HD)
    message = jnp.concatenate([kept, got, packed_rows], axis=0)
    packed = jnp.stack([message] + [to_group(message, k) for k in range(1, N_FSDP)])

    def slot_of(z_step, x_flip):
        return (2 * ((z + z_step) % 4) + (x ^ x_flip)) ^ group

    def heads_of(*pairs):
        return jnp.stack([slot_of(*pair) for pair in pairs]).astype(jnp.int32)

    def partial(picked, start, rows, tile):
        return partial_heads(prefix_states, other_states, packed, picked, start, rows, tile)

    half = Z_FIRST // 2
    far, up, down, own = (heads_of((r, 0), (r, 1)) for r in (2, 1, 3, 0))
    order = (2, 1, 3, 0)
    x_away = partial(heads_of(*((r, 1) for r in order)), Z_FIRST, slots - Z_FIRST, X_TILE)
    x_in = to_x(x_away)
    z_parts = [
        partial(picked, start, half, Z_TILE)
        for picked in (far, up, down, own)
        for start in (0, half)
    ]
    sum_a, sum_b = reduce_over_z(*z_parts)
    x_own = partial(heads_of(*((r, 0) for r in order)), Z_FIRST, slots - Z_FIRST, X_TILE)

    half_x = (slots - Z_FIRST) // 2
    x_parts = []
    for j in range(4):
        for low in (0, half_x):
            cut = lambda block: block[low : low + half_x, j * HD : (j + 1) * HD]
            x_parts.append(add(cut(x_own), cut(x_in)))
    x_sum_a, x_sum_b = reduce_over_z(*x_parts)
    z_sum = [jnp.concatenate(pair, 0) for pair in zip(sum_a, sum_b)]
    z_away = add(*(block[:, HD:] for block in z_sum))
    z_own = add(*(block[:, :HD] for block in z_sum))
    z_in = to_x(z_away)

    terms = fresh_terms(group.reshape(1).astype(jnp.int32), packed, w_query, w_keyvalue)
    fresh = transpose_mesh(
        jnp.sum(lax.all_to_all(terms, "tp", 0, 0, tiled=True), axis=0)
    )
    seq_lengths = lengths[0]
    positions = (
        jnp.repeat(seq_lengths, STEPS) + jnp.tile(jnp.arange(STEPS, dtype=jnp.int32), NSEQ)
    ).astype(f32)
    cosine, sine = tables(positions)
    fresh_cos = jnp.where(holds_keys, cosine, 1.0)
    fresh_sin = jnp.where(holds_keys, sine, 0.0)
    fresh_mine = rotate(fresh[:, 512:], fresh_cos, fresh_sin).astype(bf16)
    fresh_other = to_core(fresh_mine)
    query = (
        rotate(fresh[:, :512].reshape(ROWS, 4, HD), cosine[:, None, :], sine[:, None, :])
        .astype(bf16)
        .reshape(4 * ROWS, HD)
    )

    slot_cos, slot_sin = tables(jnp.arange(L, dtype=f32))
    slot_cos = jnp.where(holds_keys, slot_cos, 1.0)
    slot_sin = jnp.where(holds_keys, slot_sin, 0.0)
    cache_mine = finish_cache(z_own, z_in, add(*x_sum_a), add(*x_sum_b), slot_cos, slot_sin)
    cache_other = to_core(cache_mine)
    info = jnp.concatenate([seq_lengths, core.reshape(1).astype(jnp.int32)])
    attended = attend(info, cache_mine, cache_other, fresh_mine, fresh_other, query)
    attended = attended.reshape(1, ROWS, 512)
    gathered = lax.all_to_all(
        jnp.broadcast_to(attended, (N_FSDP, ROWS, 512)), "fsdp", 0, 0, tiled=True
    )
    output = output_terms(gathered, w_output)
    total = jnp.sum(lax.all_to_all(output, "tp", 0, 0, tiled=True), axis=0)
    mixed = transpose_mesh(total.astype(bf16))
    return cache_mine, mixed


def solution(mesh):
    in_specs = (
        P("fsdp", "tp"),
        P("fsdp", "tp"),
        P("tp", "fsdp"),
        P("tp", "fsdp"),
        P("tp", "fsdp"),
        P("fsdp", None),
    )
    out_specs = (P("fsdp", "tp"), P("fsdp", "tp"))
    return jax.shard_map(body, mesh=mesh, in_specs=in_specs, out_specs=out_specs, check_vma=False)
```

```python
import jax
import jax.numpy as jnp
from jax import lax
from jax.experimental import pallas as pl
from jax.experimental.pallas import tpu as pltpu
from jax.sharding import PartitionSpec as P


HD = 128
NSEQ = 4
L = 1024
STEPS = 4
N_FSDP = 8
N_TP = 16
ROWS = NSEQ * STEPS


theta_base = 500000.0
masked_score = -1e30
both = ("fsdp", "tp")
f32 = jnp.float32
bf16 = jnp.bfloat16

Z_FIRST = 2560
Z_TILE = 640


def route(move):
    pairs = []
    for f in range(N_FSDP):
        for t in range(N_TP):
            a, b = move(f, t)
            pairs.append((f * N_TP + t, a * N_TP + b))
    return pairs


def to_core(block):
    return lax.ppermute(block, both, route(lambda f, t: (f, t ^ 1)))


def to_x(block):
    return lax.ppermute(block, both, route(lambda f, t: (f, t ^ 2)))


def to_z(block, step):
    return lax.ppermute(
        block, both, route(lambda f, t: (f, (((t >> 2) + step) % 4) << 2 | (t & 3)))
    )


def to_group(block, flip):
    return lax.ppermute(block, both, route(lambda f, t: (f ^ flip, t)))


def transpose_mesh(block):
    return lax.ppermute(block, both, route(lambda f, t: (t >> 1, 2 * f + (t & 1))))


def output_owner(block):
    return lax.ppermute(
        block, both, route(lambda f, t: ((t >> 3) * 4 + (f & 3), (f >> 2) * 8 + (t & 7)))
    )


def pick_heads(slots, base, messages, merged):
    for j in range(4):
        for k in range(N_FSDP):

            @pl.when(slots[base + j] == k)
            def _():
                merged[:, j * HD : (j + 1) * HD] = messages[k][: merged.shape[0], :]


def product(x1, x2, merged):
    depth = x1.shape[1]
    total = jnp.dot(x1[...], merged[:depth, :], preferred_element_type=f32)
    total = total + jnp.dot(x2[...], merged[depth:, :], preferred_element_type=f32)
    return total.astype(bf16)


def z_kernel(slots, x1, x2, *rest):
    messages, (a0, a1, b0, b1, merged) = rest[:N_FSDP], rest[-5:]
    i = pl.program_id(0)
    a_tiles = pl.num_programs(0) // 2
    region = jnp.where(i >= a_tiles, 1, 0)

    @pl.when((i == 0) | (i == a_tiles))
    def _():
        pick_heads(slots, region * 4, messages, merged)

    total = product(x1, x2, merged)

    @pl.when(region == 0)
    def _():
        a0[...] = total[:, : 2 * HD]
        a1[...] = total[:, 2 * HD :]

    @pl.when(region == 1)
    def _():
        b0[...] = total[:, : 2 * HD]
        b1[...] = total[:, 2 * HD :]


def x_kernel(slots, x1, x2, *rest):
    messages, (far, merged) = rest[:N_FSDP], rest[-2:]

    @pl.when(pl.program_id(0) == 0)
    def _():
        pick_heads(slots, 8, messages, merged)

    far[...] = product(x1, x2, merged)


def x_merge_kernel(slots, x1, x2, *rest):
    messages, rest = rest[:N_FSDP], rest[N_FSDP:]
    addend, w_query, w_keyvalue = rest[:3]
    parts, (terms, merged, rows_ref) = rest[3:11], rest[11:]
    i = pl.program_id(0)

    @pl.when(i == 0)
    def _():
        pick_heads(slots, 8, messages, merged)

    depth = x1.shape[1]
    total = jnp.dot(x1[...], merged[:depth, :], preferred_element_type=f32)
    total = total + jnp.dot(x2[...], merged[depth:, :], preferred_element_type=f32)
    total = (total + addend[...].astype(f32)).astype(bf16)
    for side in range(2):

        @pl.when(i == side)
        def _():
            for j in range(4):
                parts[4 * side + j][...] = total[:, j * HD : (j + 1) * HD]

    @pl.when(i == 1)
    def _():
        fresh_rows(slots[12], messages, w_query, w_keyvalue, terms, rows_ref)


def fresh_rows(group, messages, w_query, w_keyvalue, out, rows_ref):
    for k in range(N_FSDP):
        low = pl.multiple_of((group ^ k) * ROWS, ROWS)
        for j in range(4):
            rows_ref[pl.ds(low, ROWS), j * HD : (j + 1) * HD] = messages[k][
                1024 + j * ROWS : 1024 + (j + 1) * ROWS, :
            ]
    rows = rows_ref[...]
    query = jnp.dot(rows, w_query[...], preferred_element_type=f32)
    keyvalue = jnp.dot(rows, w_keyvalue[...], preferred_element_type=f32)
    for a in range(N_FSDP):
        for h in range(2):
            low = a * ROWS
            out[2 * a + h, :, :512] = query[low : low + ROWS, h * 512 : (h + 1) * 512]
            out[2 * a + h, :, 512:] = keyvalue[low : low + ROWS, h * HD : (h + 1) * HD]


def whole(shape):
    return pl.BlockSpec(shape, lambda i, s: (0,) * len(shape))


def cost(rows, depth):
    return pl.CostEstimate(
        flops=4 * rows * depth * 4 * HD,
        bytes_accessed=2 * (2 * rows * depth + rows * 4 * HD),
        transcendentals=0,
    )


def z_heads(x1, x2, messages, slots, ready=()):
    depth = x1.shape[1]
    half = Z_FIRST // 2
    a_tiles = half // Z_TILE
    x_spec = pl.BlockSpec((Z_TILE, depth), lambda i, s: (i, 0))
    a_spec = pl.BlockSpec((Z_TILE, 2 * HD), lambda i, s: (jnp.minimum(i, a_tiles - 1), 0))
    b_spec = pl.BlockSpec((Z_TILE, 2 * HD), lambda i, s: (jnp.maximum(i - a_tiles, 0), 0))
    return pl.pallas_call(
        z_kernel,
        out_shape=[jax.ShapeDtypeStruct((half, 2 * HD), bf16)] * 4,
        grid_spec=pltpu.PrefetchScalarGridSpec(
            num_scalar_prefetch=1,
            grid=(2 * a_tiles,),
            in_specs=[x_spec, x_spec]
            + [whole(m.shape) for m in messages]
            + [pl.BlockSpec(memory_space=pl.ANY)] * len(ready),
            out_specs=[a_spec, a_spec, b_spec, b_spec],
            scratch_shapes=[pltpu.VMEM((2 * depth, 4 * HD), bf16)],
        ),
        cost_estimate=cost(Z_FIRST, depth),
        name="z_heads",
    )(slots, x1, x2, *messages, *ready)


def x_rows(depth, half):
    return pl.BlockSpec(
        (pl.Element(half), pl.Element(depth)), lambda i, s: (pl.multiple_of(Z_FIRST + half * i, 256), 0)
    )


def x_heads(x1, x2, messages, slots, ready):
    count, depth = x1.shape
    rows = count - Z_FIRST
    half = rows // 2
    return pl.pallas_call(
        x_kernel,
        out_shape=jax.ShapeDtypeStruct((rows, 4 * HD), bf16),
        grid_spec=pltpu.PrefetchScalarGridSpec(
            num_scalar_prefetch=1,
            grid=(2,),
            in_specs=[x_rows(depth, half)] * 2
            + [whole(m.shape) for m in messages]
            + [pl.BlockSpec(memory_space=pl.ANY)] * len(ready),
            out_specs=pl.BlockSpec((half, 4 * HD), lambda i, s: (i, 0)),
            scratch_shapes=[pltpu.VMEM((2 * depth, 4 * HD), bf16)],
        ),
        cost_estimate=cost(rows, depth),
        name="x_heads",
    )(slots, x1, x2, *messages, *ready)


def x_merge(x1, x2, messages, slots, addend, w_query, w_keyvalue):
    count, depth = x1.shape
    rows = count - Z_FIRST
    half = rows // 2
    terms = (N_TP, ROWS, 640)
    return pl.pallas_call(
        x_merge_kernel,
        out_shape=[jax.ShapeDtypeStruct((half, HD), bf16)] * 8
        + [jax.ShapeDtypeStruct(terms, f32)],
        grid_spec=pltpu.PrefetchScalarGridSpec(
            num_scalar_prefetch=1,
            grid=(2,),
            in_specs=[x_rows(depth, half)] * 2
            + [whole(m.shape) for m in messages]
            + [pl.BlockSpec((half, 4 * HD), lambda i, s: (i, 0))]
            + [whole(w_query.shape), whole(w_keyvalue.shape)],
            out_specs=[whole((half, HD))] * 8 + [whole(terms)],
            scratch_shapes=[
                pltpu.VMEM((2 * depth, 4 * HD), bf16),
                pltpu.VMEM((N_FSDP * ROWS, 512), bf16),
            ],
        ),
        cost_estimate=cost(rows, depth),
        name="x_merge",
    )(slots, x1, x2, *messages, addend, w_query, w_keyvalue)


def message_kernel(kind, w_keyvalue, got, new_states, out):
    depth = got.shape[0]
    out[:depth, :] = jnp.where(kind[0] == 0, w_keyvalue[:, :HD], w_keyvalue[:, HD:])
    out[depth : 2 * depth, :] = got[...]
    for j in range(4):
        low = 2 * depth + j * ROWS
        out[low : low + ROWS, :] = new_states[:, j * HD : (j + 1) * HD]


def pack_message(kind, w_keyvalue, got, new_states):
    vmem = pl.BlockSpec(memory_space=pltpu.VMEM)
    return pl.pallas_call(
        message_kernel,
        out_shape=jax.ShapeDtypeStruct((2 * got.shape[0] + 4 * ROWS, HD), bf16),
        in_specs=[pl.BlockSpec(memory_space=pltpu.SMEM)] + [vmem] * 3,
        out_specs=vmem,
        name="pack_message",
    )(kind, w_keyvalue, got, new_states)


def output_kernel(group, mine, other, w0, w1, w2, w3, out):
    low, high = group[0] & 3, group[0] >> 2
    rows = jnp.concatenate([mine[...], other[...]], axis=0)
    for k, weight in enumerate((w0, w1, w2, w3)):
        total = jnp.dot(rows, weight[...], preferred_element_type=f32).astype(bf16)
        for j in range(2):
            for h in range(2):
                at = (high ^ j) * 8 + (low ^ k) * 2 + h
                out[at] = total[j * ROWS : (j + 1) * ROWS, h * 512 : (h + 1) * 512]


def output_terms(group, mine, other, weights):
    vmem = pl.BlockSpec(memory_space=pltpu.VMEM)
    return pl.pallas_call(
        output_kernel,
        out_shape=jax.ShapeDtypeStruct((N_TP, ROWS, 512), bf16),
        in_specs=[pl.BlockSpec(memory_space=pltpu.SMEM)] + [vmem] * 6,
        out_specs=vmem,
        name="output_terms",
    )(group, mine, other, *weights)


def finish_kernel(*refs):
    cosine, sine, out = refs[14:]
    step = 256
    base = 0
    for addends in (refs[:4], refs[4:8], refs[8:11], refs[11:14]):
        count = addends[0].shape[0]
        for low in range(0, count, step):
            rows = slice(low, low + step)
            total = sum(ref[rows, :].astype(f32) for ref in addends)
            at = base + low
            table = slice(at % L, at % L + step)
            total = total * cosine[table, :] + pltpu.roll(total, HD // 2, 1) * sine[table, :]
            out[at : at + step, :] = total.astype(bf16)
        base += count


def finish_cache(pieces, cosine, sine):
    arrays = [block for block, _, _ in pieces] + [cosine, sine]
    specs = [
        pl.BlockSpec((rows, HD), lambda i, at=at: at) for (_, rows, at) in pieces
    ] + [pl.BlockSpec((L, HD), lambda i: (0, 0))] * 2
    return pl.pallas_call(
        finish_kernel,
        grid=(1,),
        out_shape=jax.ShapeDtypeStruct((NSEQ * L, HD), bf16),
        in_specs=specs,
        out_specs=pl.BlockSpec((NSEQ * L, HD), lambda i: (0, 0)),
        name="finish_cache",
    )(*arrays)


def attention_kernel(info, mine, other, fresh_mine, fresh_other, query, out):
    holds_keys = info[NSEQ] == 0
    scale = HD ** (-0.5)
    fresh_keys = jnp.where(holds_keys, fresh_mine[...], fresh_other[...])
    fresh_values = jnp.where(holds_keys, fresh_other[...], fresh_mine[...])
    for s in range(NSEQ):
        part = slice(s * L, (s + 1) * L)
        keys = jnp.where(holds_keys, mine[part, :], other[part, :])
        values = jnp.where(holds_keys, other[part, :], mine[part, :])
        rows = query[s * 16 : (s + 1) * 16, :]
        last = (((1,), (1,)), ((), ()))
        scores = lax.dot_general(rows, keys, last, preferred_element_type=f32) * scale
        slot = lax.broadcasted_iota(jnp.int32, scores.shape, 1)
        scores = jnp.where(slot < info[s], scores, masked_score)
        fresh = lax.dot_general(rows, fresh_keys, last, preferred_element_type=f32) * scale
        row = lax.broadcasted_iota(jnp.int32, fresh.shape, 0)
        column = lax.broadcasted_iota(jnp.int32, fresh.shape, 1)
        step = column - s * STEPS
        live = (step >= 0) & (step <= (row >> 2))
        fresh = jnp.where(live, fresh, masked_score)
        top = jnp.maximum(
            jnp.max(scores, axis=1, keepdims=True), jnp.max(fresh, axis=1, keepdims=True)
        )
        weight = jnp.exp(scores - top)
        fresh_weight = jnp.exp(fresh - top)
        denominator = jnp.sum(weight, axis=1, keepdims=True) + jnp.sum(
            fresh_weight, axis=1, keepdims=True
        )
        numerator = jnp.dot(weight.astype(bf16), values, preferred_element_type=f32)
        numerator = numerator + jnp.dot(
            fresh_weight.astype(bf16), fresh_values, preferred_element_type=f32
        )
        out[s * 16 : (s + 1) * 16, :] = (numerator / denominator).astype(bf16)


def attend(info, mine, other, fresh_mine, fresh_other, query):
    vmem = pl.BlockSpec(memory_space=pltpu.VMEM)
    return pl.pallas_call(
        attention_kernel,
        out_shape=jax.ShapeDtypeStruct((64, HD), bf16),
        in_specs=[pl.BlockSpec(memory_space=pltpu.SMEM)] + [vmem] * 5,
        out_specs=vmem,
        name="attend",
    )(info, mine, other, fresh_mine, fresh_other, query)


def rotate(values, cosine, sine):
    return values * cosine + jnp.roll(values, HD // 2, axis=-1) * sine


def tables(positions):
    half = HD // 2
    frequency = theta_base ** (-2.0 * jnp.arange(half, dtype=f32) / HD)
    angles = positions[:, None] * frequency[None, :]
    cosine, sine = jnp.cos(angles), jnp.sin(angles)
    return jnp.concatenate([cosine, cosine], 1), jnp.concatenate([-sine, sine], 1)


def add(*blocks):
    total = blocks[0].astype(f32)
    for block in blocks[1:]:
        total = total + block.astype(f32)
    return total.astype(bf16)


def reduce_over_z(far_a, far_b, up_a, up_b, down_a, down_b):
    in_far_a = to_z(far_a, 1)
    in_far_b = to_z(far_b, -1)
    in_up_b = to_z(up_b, 1)
    in_down_a = to_z(down_a, -1)
    merged_a = add(up_a, in_far_a)
    merged_b = add(down_b, in_far_b)
    in_up_a = to_z(merged_a, 1)
    in_down_b = to_z(merged_b, -1)
    return in_down_a, in_up_a, in_up_b, in_down_b


def relay(message):
    far = to_group(message, 2)
    beside = to_group(message, 4)
    one = to_group(message, 1)
    three = to_group(message, 3)
    five = to_group(beside, 1)
    seven = to_group(beside, 3)
    six = to_group(far, 4)
    return [message, one, far, three, beside, five, six, seven]


def body(prefix_states, new_states, w_query, w_keyvalue, w_output, lengths):
    group = lax.axis_index("fsdp")
    me = lax.axis_index("tp")
    z, x, core = me >> 2, (me >> 1) & 1, me & 1
    slots = prefix_states.shape[0]
    holds_keys = core == 0

    lower, upper = w_keyvalue[:, :HD], w_keyvalue[:, HD:]
    got = to_core(jnp.where(holds_keys, upper, lower))
    other_states = to_core(prefix_states)
    kind = core.reshape(1).astype(jnp.int32)
    messages = relay(pack_message(kind, w_keyvalue, got, new_states))

    slot_cos, slot_sin = tables(jnp.arange(L, dtype=f32))
    slot_cos = jnp.where(holds_keys, slot_cos, 1.0)
    slot_sin = jnp.where(holds_keys, slot_sin, 0.0)

    def slot_of(z_step, x_flip):
        return (2 * ((z + z_step) % 4) + (x ^ x_flip)) ^ group

    far, up, down, own = ([(r, 0), (r, 1)] for r in (2, 1, 3, 0))
    order = (2, 1, 3, 0)

    def picked(*pairs):
        return jnp.stack([slot_of(*pair) for pair in pairs] + [group]).astype(jnp.int32)

    first = picked(*far, *down, *far, *up, *((r, 1) for r in order))
    second = picked(*up, *own, *down, *own, *((r, 0) for r in order))
    states = (prefix_states, other_states, messages)
    x_away = x_heads(*states, first, (slot_cos, slot_sin))
    x_in = to_x(x_away)
    far_a, down_a, far_b, up_b = z_heads(*states, first)
    up_a, own_a, down_b, own_b = z_heads(*states, second)
    in_down_a, in_up_a, in_up_b, in_down_b = reduce_over_z(
        far_a, far_b, up_a, up_b, down_a, down_b
    )
    *x_parts, terms = x_merge(*states, second, x_in, w_query, w_keyvalue)
    far_xa, up_xa, down_xa, own_xa, far_xb, up_xb, down_xb, own_xb = x_parts
    x_down_a, x_up_a, x_up_b, x_down_b = reduce_over_z(
        far_xa, far_xb, up_xa, up_xb, down_xa, down_xb
    )
    half = Z_FIRST // 2
    half_x = (slots - Z_FIRST) // 2
    x_in_a = to_x(add(own_a[:, HD:], in_down_a[:, HD:], in_up_a[:, HD:]))
    x_in_b = to_x(add(own_b[:, HD:], in_up_b[:, HD:], in_down_b[:, HD:]))
    outputs = [w_output]
    for k in (1, 2, 3):
        outputs.append(to_group(w_output, k))

    fresh = lax.all_to_all(terms, "tp", 0, 0, tiled=True)
    fresh = transpose_mesh(jnp.sum(fresh, axis=0))
    seq_lengths = lengths[0]
    positions = (
        jnp.repeat(seq_lengths, STEPS) + jnp.tile(jnp.arange(STEPS, dtype=jnp.int32), NSEQ)
    ).astype(f32)
    cosine, sine = tables(positions)
    fresh_cos = jnp.where(holds_keys, cosine, 1.0)
    fresh_sin = jnp.where(holds_keys, sine, 0.0)
    fresh_mine = rotate(fresh[:, 512:], fresh_cos, fresh_sin).astype(bf16)
    fresh_other = to_core(fresh_mine)
    query = (
        rotate(fresh[:, :512].reshape(ROWS, 4, HD), cosine[:, None, :], sine[:, None, :])
        .astype(bf16)
        .reshape(4 * ROWS, HD)
    )

    pieces = [(block, half, (0, 0)) for block in (own_a, in_down_a, in_up_a, x_in_a)]
    pieces += [(block, half, (0, 0)) for block in (own_b, in_up_b, in_down_b, x_in_b)]
    pieces += [(block, half_x, (0, 0)) for block in (own_xa, x_down_a, x_up_a)]
    pieces += [(block, half_x, (0, 0)) for block in (own_xb, x_up_b, x_down_b)]
    cache_mine = finish_cache(pieces, slot_cos, slot_sin)
    cache_other = to_core(cache_mine)
    info = jnp.concatenate([seq_lengths, core.reshape(1).astype(jnp.int32)])
    attended = attend(info, cache_mine, cache_other, fresh_mine, fresh_other, query)
    attended = attended.reshape(ROWS, 512)
    beside = to_group(attended, 4)
    output = output_terms(group.reshape(1).astype(jnp.int32), attended, beside, outputs)
    total = jnp.sum(lax.all_to_all(output, "tp", 0, 0, tiled=True).astype(f32), axis=0)
    mixed = output_owner(total.astype(bf16))
    return cache_mine, mixed


def solution(mesh):
    in_specs = (
        P("fsdp", "tp"),
        P("fsdp", "tp"),
        P("tp", "fsdp"),
        P("tp", "fsdp"),
        P("tp", "fsdp"),
        P("fsdp", None),
    )
    out_specs = (P("fsdp", "tp"), P("fsdp", "tp"))
    return jax.shard_map(
        body, mesh=mesh, in_specs=in_specs, out_specs=out_specs, check_vma=False
    )
```

```python
import jax
import jax.numpy as jnp
import numpy as np
from jax import lax
from jax.experimental import pallas as pl
from jax.experimental.pallas import tpu as pltpu
from jax.sharding import PartitionSpec as P


HD = 128
NSEQ = 4
L = 1024
STEPS = 4
N_FSDP = 8
N_TP = 16
ROWS = NSEQ * STEPS


theta_base = 500000.0
masked_score = -1e30
both = ("fsdp", "tp")
f32 = jnp.float32
bf16 = jnp.bfloat16

Z_FIRST = 2560
Z_TILE = 640


def route(move):
    pairs = []
    for f in range(N_FSDP):
        for t in range(N_TP):
            a, b = move(f, t)
            pairs.append((f * N_TP + t, a * N_TP + b))
    return pairs


def to_core(block):
    return lax.ppermute(block, both, route(lambda f, t: (f, t ^ 1)))


def to_x(block):
    return lax.ppermute(block, both, route(lambda f, t: (f, t ^ 2)))


def to_z(block, step):
    return lax.ppermute(
        block, both, route(lambda f, t: (f, (((t >> 2) + step) % 4) << 2 | (t & 3)))
    )


def to_group(block, flip):
    return lax.ppermute(block, both, route(lambda f, t: (f ^ flip, t)))


def transpose_mesh(block):
    return lax.ppermute(block, both, route(lambda f, t: (t >> 1, 2 * f + (t & 1))))


def output_owner(block):
    return lax.ppermute(
        block, both, route(lambda f, t: ((t >> 3) * 4 + (f & 3), (f >> 2) * 8 + (t & 7)))
    )


def pick_heads(slots, base, messages, merged):
    for j in range(4):
        for k in range(N_FSDP):

            @pl.when(slots[base + j] == k)
            def _():
                merged[:, j * HD : (j + 1) * HD] = messages[k][: merged.shape[0], :]


def product(x1, x2, merged):
    depth = x1.shape[1]
    total = jnp.dot(x1[...], merged[:depth, :], preferred_element_type=f32)
    total = total + jnp.dot(x2[...], merged[depth:, :], preferred_element_type=f32)
    return total.astype(bf16)


def z_kernel(slots, x1, x2, *rest):
    messages, (a0, a1, b0, b1, merged) = rest[:N_FSDP], rest[-5:]
    i = pl.program_id(0)
    a_tiles = pl.num_programs(0) // 2
    region = jnp.where(i >= a_tiles, 1, 0)

    @pl.when((i == 0) | (i == a_tiles))
    def _():
        pick_heads(slots, region * 4, messages, merged)

    total = product(x1, x2, merged)

    @pl.when(region == 0)
    def _():
        a0[...] = total[:, : 2 * HD]
        a1[...] = total[:, 2 * HD :]

    @pl.when(region == 1)
    def _():
        b0[...] = total[:, : 2 * HD]
        b1[...] = total[:, 2 * HD :]


def x_kernel(slots, x1, x2, *rest):
    messages, (far, merged) = rest[:N_FSDP], rest[-2:]

    @pl.when(pl.program_id(0) == 0)
    def _():
        pick_heads(slots, 8, messages, merged)

    far[...] = product(x1, x2, merged)


def x_merge_kernel(slots, x1, x2, *rest):
    messages, rest = rest[:N_FSDP], rest[N_FSDP:]
    addend, parts, merged = rest[0], rest[1:9], rest[9]
    i = pl.program_id(0)

    @pl.when(i == 0)
    def _():
        pick_heads(slots, 8, messages, merged)

    depth = x1.shape[1]
    total = jnp.dot(x1[...], merged[:depth, :], preferred_element_type=f32)
    total = total + jnp.dot(x2[...], merged[depth:, :], preferred_element_type=f32)
    total = (total + addend[...].astype(f32)).astype(bf16)
    for side in range(2):

        @pl.when(i == side)
        def _():
            for j in range(4):
                parts[4 * side + j][...] = total[:, j * HD : (j + 1) * HD]


def fresh_kernel(group, b0, b1, b2, b3, w_query, w_keyvalue, out, rows_ref):
    beside = (b0, b1, b2, b3)
    for k in range(N_FSDP):
        low = pl.multiple_of((group[0] ^ k) * ROWS, ROWS)
        rows_ref[pl.ds(low, ROWS), :] = beside[k & 3][k >> 2]
    rows = rows_ref[...]
    query = jnp.dot(rows, w_query[...], preferred_element_type=f32)
    keyvalue = jnp.dot(rows, w_keyvalue[...], preferred_element_type=f32)
    for a in range(N_FSDP):
        for h in range(2):
            low = a * ROWS
            out[2 * a + h, :, :512] = query[low : low + ROWS, h * 512 : (h + 1) * 512]
            out[2 * a + h, :, 512:] = keyvalue[low : low + ROWS, h * HD : (h + 1) * HD]


def fresh_terms(group, beside, w_query, w_keyvalue):
    vmem = pl.BlockSpec(memory_space=pltpu.VMEM)
    return pl.pallas_call(
        fresh_kernel,
        out_shape=jax.ShapeDtypeStruct((N_TP, ROWS, 640), f32),
        in_specs=[pl.BlockSpec(memory_space=pltpu.SMEM)] + [vmem] * 6,
        out_specs=vmem,
        scratch_shapes=[pltpu.VMEM((N_FSDP * ROWS, 512), bf16)],
        name="fresh_terms",
    )(group, *beside, w_query, w_keyvalue)


def whole(shape):
    return pl.BlockSpec(shape, lambda i, s: (0,) * len(shape))


def cost(rows, depth):
    return pl.CostEstimate(
        flops=4 * rows * depth * 4 * HD,
        bytes_accessed=2 * (2 * rows * depth + rows * 4 * HD),
        transcendentals=0,
    )


def z_heads(x1, x2, messages, slots, ready=()):
    depth = x1.shape[1]
    half = Z_FIRST // 2
    a_tiles = half // Z_TILE
    x_spec = pl.BlockSpec((Z_TILE, depth), lambda i, s: (i, 0))
    a_spec = pl.BlockSpec((Z_TILE, 2 * HD), lambda i, s: (jnp.minimum(i, a_tiles - 1), 0))
    b_spec = pl.BlockSpec((Z_TILE, 2 * HD), lambda i, s: (jnp.maximum(i - a_tiles, 0), 0))
    return pl.pallas_call(
        z_kernel,
        out_shape=[jax.ShapeDtypeStruct((half, 2 * HD), bf16)] * 4,
        grid_spec=pltpu.PrefetchScalarGridSpec(
            num_scalar_prefetch=1,
            grid=(2 * a_tiles,),
            in_specs=[x_spec, x_spec]
            + [whole(m.shape) for m in messages]
            + [pl.BlockSpec(memory_space=pl.ANY)] * len(ready),
            out_specs=[a_spec, a_spec, b_spec, b_spec],
            scratch_shapes=[pltpu.VMEM((2 * depth, 4 * HD), bf16)],
        ),
        cost_estimate=cost(Z_FIRST, depth),
        name="z_heads",
    )(slots, x1, x2, *messages, *ready)


def x_rows(depth, half):
    return pl.BlockSpec(
        (pl.Element(half), pl.Element(depth)), lambda i, s: (pl.multiple_of(Z_FIRST + half * i, 256), 0)
    )


def x_heads(x1, x2, messages, slots):
    count, depth = x1.shape
    rows = count - Z_FIRST
    half = rows // 2
    return pl.pallas_call(
        x_kernel,
        out_shape=jax.ShapeDtypeStruct((rows, 4 * HD), bf16),
        grid_spec=pltpu.PrefetchScalarGridSpec(
            num_scalar_prefetch=1,
            grid=(2,),
            in_specs=[x_rows(depth, half)] * 2 + [whole(m.shape) for m in messages],
            out_specs=pl.BlockSpec((half, 4 * HD), lambda i, s: (i, 0)),
            scratch_shapes=[pltpu.VMEM((2 * depth, 4 * HD), bf16)],
        ),
        cost_estimate=cost(rows, depth),
        name="x_heads",
    )(slots, x1, x2, *messages)


def x_merge(x1, x2, messages, slots, addend):
    count, depth = x1.shape
    rows = count - Z_FIRST
    half = rows // 2
    return pl.pallas_call(
        x_merge_kernel,
        out_shape=[jax.ShapeDtypeStruct((half, HD), bf16)] * 8,
        grid_spec=pltpu.PrefetchScalarGridSpec(
            num_scalar_prefetch=1,
            grid=(2,),
            in_specs=[x_rows(depth, half)] * 2
            + [whole(m.shape) for m in messages]
            + [pl.BlockSpec((half, 4 * HD), lambda i, s: (i, 0))],
            out_specs=[whole((half, HD))] * 8,
            scratch_shapes=[pltpu.VMEM((2 * depth, 4 * HD), bf16)],
        ),
        cost_estimate=cost(rows, depth),
        name="x_merge",
    )(slots, x1, x2, *messages, addend)


def message_kernel(kind, w_keyvalue, got, out):
    depth = got.shape[0]
    out[:depth, :] = jnp.where(kind[0] == 0, w_keyvalue[:, :HD], w_keyvalue[:, HD:])
    out[depth:, :] = got[...]


def pack_message(kind, w_keyvalue, got):
    vmem = pl.BlockSpec(memory_space=pltpu.VMEM)
    return pl.pallas_call(
        message_kernel,
        out_shape=jax.ShapeDtypeStruct((2 * got.shape[0], HD), bf16),
        in_specs=[pl.BlockSpec(memory_space=pltpu.SMEM)] + [vmem] * 2,
        out_specs=vmem,
        name="pack_message",
    )(kind, w_keyvalue, got)


def output_kernel(group, mine, other, w0, w1, w2, w3, out):
    low, high = group[0] & 3, group[0] >> 2
    rows = jnp.concatenate([mine[...], other[...]], axis=0)
    for k, weight in enumerate((w0, w1, w2, w3)):
        total = jnp.dot(rows, weight[...], preferred_element_type=f32).astype(bf16)
        for j in range(2):
            for h in range(2):
                at = (high ^ j) * 8 + (low ^ k) * 2 + h
                out[at] = total[j * ROWS : (j + 1) * ROWS, h * 512 : (h + 1) * 512]


def output_terms(group, mine, other, weights):
    vmem = pl.BlockSpec(memory_space=pltpu.VMEM)
    return pl.pallas_call(
        output_kernel,
        out_shape=jax.ShapeDtypeStruct((N_TP, ROWS, 512), bf16),
        in_specs=[pl.BlockSpec(memory_space=pltpu.SMEM)] + [vmem] * 6,
        out_specs=vmem,
        name="output_terms",
    )(group, mine, other, *weights)


def slot_table():
    half = HD // 2
    frequency = (theta_base ** (-2.0 * np.arange(half) / HD)).astype(np.float32)
    angles = np.arange(L, dtype=np.float32)[:, None] * frequency[None, :]
    angles = angles.astype(np.float64)
    return np.concatenate([np.cos(angles), np.sin(angles)], axis=1).astype(np.float32)


def finish_kernel(kind, *refs):
    table, out = refs[14:]
    step = 256
    lane = lax.broadcasted_iota(jnp.int32, (step, HD), 1)
    lower = lane < HD // 2

    def finish(rotated):
        base = 0
        for addends in (refs[:4], refs[4:8], refs[8:11], refs[11:14]):
            count = addends[0].shape[0]
            for low in range(0, count, step):
                rows = slice(low, low + step)
                total = sum(ref[rows, :].astype(f32) for ref in addends)
                at = base + low
                if rotated:
                    angle = table[at % L : at % L + step, :]
                    turned = pltpu.roll(angle, HD // 2, 1)
                    cosine = jnp.where(lower, angle, turned)
                    sine = jnp.where(lower, -turned, angle)
                    total = total * cosine + pltpu.roll(total, HD // 2, 1) * sine
                out[at : at + step, :] = total.astype(bf16)
            base += count

    @pl.when(kind[0] == 0)
    def _():
        finish(True)

    @pl.when(kind[0] != 0)
    def _():
        finish(False)


def finish_cache(kind, pieces, table):
    arrays = [block for block, _, _ in pieces] + [table]
    specs = [
        pl.BlockSpec((rows, HD), lambda i, s, at=at: at) for (_, rows, at) in pieces
    ] + [whole((L, HD))]
    return pl.pallas_call(
        finish_kernel,
        grid_spec=pltpu.PrefetchScalarGridSpec(
            num_scalar_prefetch=1,
            grid=(1,),
            in_specs=specs,
            out_specs=whole((NSEQ * L, HD)),
        ),
        out_shape=jax.ShapeDtypeStruct((NSEQ * L, HD), bf16),
        name="finish_cache",
    )(kind, *arrays)


def attention_kernel(info, mine, other, fresh_mine, fresh_other, query, out):
    holds_keys = info[NSEQ] == 0
    scale = HD ** (-0.5)
    fresh_keys = jnp.where(holds_keys, fresh_mine[...], fresh_other[...])
    fresh_values = jnp.where(holds_keys, fresh_other[...], fresh_mine[...])
    for s in range(NSEQ):
        part = slice(s * L, (s + 1) * L)
        keys = jnp.where(holds_keys, mine[part, :], other[part, :])
        values = jnp.where(holds_keys, other[part, :], mine[part, :])
        rows = query[s * 16 : (s + 1) * 16, :]
        last = (((1,), (1,)), ((), ()))
        scores = lax.dot_general(rows, keys, last, preferred_element_type=f32) * scale
        slot = lax.broadcasted_iota(jnp.int32, scores.shape, 1)
        scores = jnp.where(slot < info[s], scores, masked_score)
        fresh = lax.dot_general(rows, fresh_keys, last, preferred_element_type=f32) * scale
        row = lax.broadcasted_iota(jnp.int32, fresh.shape, 0)
        column = lax.broadcasted_iota(jnp.int32, fresh.shape, 1)
        step = column - s * STEPS
        live = (step >= 0) & (step <= (row >> 2))
        fresh = jnp.where(live, fresh, masked_score)
        top = jnp.maximum(
            jnp.max(scores, axis=1, keepdims=True), jnp.max(fresh, axis=1, keepdims=True)
        )
        weight = jnp.exp(scores - top)
        fresh_weight = jnp.exp(fresh - top)
        denominator = jnp.sum(weight, axis=1, keepdims=True) + jnp.sum(
            fresh_weight, axis=1, keepdims=True
        )
        numerator = jnp.dot(weight.astype(bf16), values, preferred_element_type=f32)
        numerator = numerator + jnp.dot(
            fresh_weight.astype(bf16), fresh_values, preferred_element_type=f32
        )
        out[s * 16 : (s + 1) * 16, :] = (numerator / denominator).astype(bf16)


def attend(info, mine, other, fresh_mine, fresh_other, query):
    vmem = pl.BlockSpec(memory_space=pltpu.VMEM)
    return pl.pallas_call(
        attention_kernel,
        out_shape=jax.ShapeDtypeStruct((64, HD), bf16),
        in_specs=[pl.BlockSpec(memory_space=pltpu.SMEM)] + [vmem] * 5,
        out_specs=vmem,
        name="attend",
    )(info, mine, other, fresh_mine, fresh_other, query)


def rotate(values, cosine, sine):
    return values * cosine + jnp.roll(values, HD // 2, axis=-1) * sine


def tables(positions):
    half = HD // 2
    frequency = theta_base ** (-2.0 * jnp.arange(half, dtype=f32) / HD)
    angles = positions[:, None] * frequency[None, :]
    cosine, sine = jnp.cos(angles), jnp.sin(angles)
    return jnp.concatenate([cosine, cosine], 1), jnp.concatenate([-sine, sine], 1)


def add(*blocks):
    total = blocks[0].astype(f32)
    for block in blocks[1:]:
        total = total + block.astype(f32)
    return total.astype(bf16)


def reduce_over_z(far_a, far_b, up_a, up_b, down_a, down_b):
    in_far_a = to_z(far_a, 1)
    in_far_b = to_z(far_b, -1)
    in_up_b = to_z(up_b, 1)
    in_down_a = to_z(down_a, -1)
    merged_a = add(up_a, in_far_a)
    merged_b = add(down_b, in_far_b)
    in_up_a = to_z(merged_a, 1)
    in_down_b = to_z(merged_b, -1)
    return in_down_a, in_up_a, in_up_b, in_down_b


def relay(message):
    far = to_group(message, 2)
    beside = to_group(message, 4)
    one = to_group(message, 1)
    three = to_group(message, 3)
    five = to_group(beside, 1)
    seven = to_group(beside, 3)
    six = to_group(far, 4)
    return [message, one, far, three, beside, five, six, seven]


def body(prefix_states, new_states, w_query, w_keyvalue, w_output, lengths):
    group = lax.axis_index("fsdp")
    me = lax.axis_index("tp")
    z, x, core = me >> 2, (me >> 1) & 1, me & 1
    holds_keys = core == 0

    lower, upper = w_keyvalue[:, :HD], w_keyvalue[:, HD:]
    got = to_core(jnp.where(holds_keys, upper, lower))
    other_states = to_core(prefix_states)
    kind = core.reshape(1).astype(jnp.int32)
    new_pair = jnp.stack([new_states, to_group(new_states, 4)])
    messages = relay(pack_message(kind, w_keyvalue, got))
    new_rows = [new_pair]
    for k in (1, 2, 3):
        new_rows.append(to_group(new_pair, k))
    own_group = group.reshape(1).astype(jnp.int32)
    terms = fresh_terms(own_group, new_rows, w_query, w_keyvalue)

    def slot_of(z_step, x_flip):
        return (2 * ((z + z_step) % 4) + (x ^ x_flip)) ^ group

    far, up, down, own = ([(r, 0), (r, 1)] for r in (2, 1, 3, 0))
    order = (2, 1, 3, 0)

    def picked(*pairs):
        return jnp.stack([slot_of(*pair) for pair in pairs] + [group]).astype(jnp.int32)

    first = picked(*far, *down, *far, *up, *((r, 1) for r in order))
    second = picked(*up, *own, *down, *own, *((r, 0) for r in order))
    states = (prefix_states, other_states, messages)
    x_away = x_heads(*states, first)
    x_in = to_x(x_away)
    far_a, down_a, far_b, up_b = z_heads(*states, first)
    up_a, own_a, down_b, own_b = z_heads(*states, second)
    in_down_a, in_up_a, in_up_b, in_down_b = reduce_over_z(
        far_a, far_b, up_a, up_b, down_a, down_b
    )
    x_parts = x_merge(*states, second, x_in)
    far_xa, up_xa, down_xa, own_xa, far_xb, up_xb, down_xb, own_xb = x_parts
    x_down_a, x_up_a, x_up_b, x_down_b = reduce_over_z(
        far_xa, far_xb, up_xa, up_xb, down_xa, down_xb
    )
    x_in_a = to_x(add(own_a[:, HD:], in_down_a[:, HD:], in_up_a[:, HD:]))
    x_in_b = to_x(add(own_b[:, HD:], in_up_b[:, HD:], in_down_b[:, HD:]))
    outputs = [w_output]
    for k in (1, 2, 3):
        outputs.append(to_group(w_output, k))

    fresh = lax.all_to_all(terms, "tp", 0, 0, tiled=True)
    fresh = jnp.sum(fresh, axis=0)
    fresh = transpose_mesh(fresh)
    seq_lengths = lengths[0]
    positions = (
        jnp.repeat(seq_lengths, STEPS) + jnp.tile(jnp.arange(STEPS, dtype=jnp.int32), NSEQ)
    ).astype(f32)
    cosine, sine = tables(positions)
    fresh_cos = jnp.where(holds_keys, cosine, 1.0)
    fresh_sin = jnp.where(holds_keys, sine, 0.0)
    fresh_mine = rotate(fresh[:, 512:], fresh_cos, fresh_sin).astype(bf16)
    fresh_other = to_core(fresh_mine)
    query = (
        rotate(fresh[:, :512].reshape(ROWS, 4, HD), cosine[:, None, :], sine[:, None, :])
        .astype(bf16)
        .reshape(4 * ROWS, HD)
    )

    half = Z_FIRST // 2
    half_x = own_xa.shape[0]
    pieces = [(block, half, (0, 0)) for block in (own_a, in_down_a, in_up_a, x_in_a)]
    pieces += [(block, half, (0, 0)) for block in (own_b, in_up_b, in_down_b, x_in_b)]
    pieces += [(block, half_x, (0, 0)) for block in (own_xa, x_down_a, x_up_a)]
    pieces += [(block, half_x, (0, 0)) for block in (own_xb, x_up_b, x_down_b)]
    cache_mine = finish_cache(kind, pieces, jnp.asarray(slot_table()))
    cache_other = to_core(cache_mine)
    info = jnp.concatenate([seq_lengths, core.reshape(1).astype(jnp.int32)])
    attended = attend(info, cache_mine, cache_other, fresh_mine, fresh_other, query)
    attended = attended.reshape(ROWS, 512)
    beside = to_group(attended, 4)
    output = output_terms(own_group, attended, beside, outputs)
    total = jnp.sum(lax.all_to_all(output, "tp", 0, 0, tiled=True).astype(f32), axis=0)
    mixed = output_owner(total.astype(bf16))
    return cache_mine, mixed


def solution(mesh):
    in_specs = (
        P("fsdp", "tp"),
        P("fsdp", "tp"),
        P("tp", "fsdp"),
        P("tp", "fsdp"),
        P("tp", "fsdp"),
        P("fsdp", None),
    )
    out_specs = (P("fsdp", "tp"), P("fsdp", "tp"))
    return jax.shard_map(
        body, mesh=mesh, in_specs=in_specs, out_specs=out_specs, check_vma=False
    )
```
